32 devices in a mesh: strike: 8 (over y, x, core), dip: 4 (over z).
Axes of the slice: x: 2, y: 2, z: 4, core: 2. Of those that a mesh axis runs over, the one named last changes fastest.
Arguments:
- slip: float32 [8192, 2048], P('strike', 'dip'), may hold values from -4 to 8
- slip_rate: float32 [8192, 2048], P('strike', 'dip'), may hold values from -6 to 6
- state: float32 [8192, 2048], P('strike', 'dip'), may hold values from -1 to 1
- loading: float32 [8192, 2048], P('strike', 'dip'), may hold values from -8 to 8
- normal_stress: float32 [8192, 2048], P('strike', 'dip'), may hold values from 0.5 to 2
- patch: int32 [8192, 2048], P('strike', 'dip'), may hold values from 0 to 3
- rate_coef: float32 [4], replicated, may hold values from 0.3 to 1
- state_coef: float32 [4], replicated, may hold values from 0.3 to 1
- slip_scale: float32 [4], replicated, may hold values from 0.5 to 2
- kernel: bfloat16 [16, 2048, 8192], P(None, ('strike', 'dip')), may hold values from -1.5 to 1.5
- history: bfloat16 [16, 2, 2048, 8192], P(None, None, ('strike', 'dip')), may hold values from -6 to 6
Outputs:
- new_rate: float32 [8192, 2048], P('strike', 'dip')
- new_state: float32 [8192, 2048], P('strike', 'dip')
- transfer_stress: float32 [8192, 2048], P('strike', 'dip')
- rate_modes: bfloat16 [2, 2048, 8192], P(None, ('strike', 'dip'))
The draws below stay inside these ranges and needn't reach their ends.
All inputs are finite; a program needn't handle non-finite values.
Results may differ from the reference program's by a relative error of at most 0.001.
Values sent between devices are 32-bit elements; how exact they have to be, the bound alone decides.
A program may use at most 192 MiB of HBM per device.

```python
import math
import jax
import jax.numpy as jnp

NX = 8192
NY = 2048
HIST = 16
PATCHES = 4
NEWTON = 8


def draw_slip(key, part):
    base = jax.random.fold_in(key, 4711)
    keys = jax.random.split(base, 6)
    along_x = jnp.arange(NX, dtype=jnp.float32)[:, None] / NX
    along_y = jnp.arange(NY, dtype=jnp.float32)[None, :] / NY
    wave_a = jax.random.randint(keys[0], (), 1, 4).astype(jnp.float32)
    wave_b = jax.random.randint(keys[1], (), 1, 3).astype(jnp.float32)
    phase_a = jax.random.uniform(keys[2], (), jnp.float32, 0.0, 2.0 * math.pi)
    phase_b = jax.random.uniform(keys[3], (), jnp.float32, 0.0, 2.0 * math.pi)
    rough = jnp.clip(jax.random.normal(keys[4], (NX, NY), jnp.float32), -4.0, 4.0)
    level = jax.random.uniform(keys[5], (), jnp.float32, 1.5, 2.5)
    amp_a = 0.8
    amp_b = 0.5
    smooth = level + amp_a * jnp.cos(2.0 * math.pi * wave_a * along_x + phase_a) + amp_b * jnp.cos(2.0 * math.pi * wave_b * along_y + phase_b)
    return (rough + smooth).astype(jnp.float32)


def with_ends(values, rng, low, high):
    index_at = [jax.random.randint(jax.random.fold_in(rng, axis), (), 0, length) for axis, length in enumerate(values.shape)]
    longest = values.shape.index(max(values.shape))
    beside = index_at[:longest] + [(index_at[longest] + 1) % values.shape[longest]] + index_at[longest + 1:]
    return values.at[tuple(index_at)].set(low).at[tuple(beside)].set(high)


def steps_of(key, shape, cuts, low, largest):
    loudness = 1.0
    for dim, parts in cuts:
        steps = jax.random.uniform(jax.random.fold_in(jax.random.fold_in(key, 6), dim), (parts,), jnp.float32, low / len(cuts), largest / len(cuts))
        loudness = loudness * jnp.repeat(jnp.exp(steps), shape[dim] // parts).reshape((-1,) + (1,) * (len(shape) - 1 - dim))
    return loudness


def bell_draw(key, extent, width, most, cuts=(), kind=jnp.bfloat16):
    entries = width * jax.random.normal(key, extent, jnp.float32)
    if cuts:
        entries = entries * steps_of(key, extent, cuts, -0.22, 0.18)
    return jnp.clip(entries, -most, most).astype(kind)


def setup_inputs(seed: int = 0) -> dict:
    splits = jax.random.split(jax.random.key(seed), 12)
    return {
        "slip": draw_slip(jax.random.fold_in(splits[11], 71), 0),
        "slip_rate": bell_draw(splits[1], (NX, NY), 1.0, 6.0, ((0, 8), (1, 4)), jnp.float32),
        "state": jnp.clip(jax.random.uniform(splits[2], (NX, NY), jnp.float32, -1.0, 1.0) * steps_of(splits[2], (NX, NY), ((0, 8), (1, 4)), -0.4, 0.0), -1.0, 1.0),
        "loading": bell_draw(splits[3], (NX, NY), 2.0, 8.0, ((0, 8), (1, 4)), jnp.float32),
        "normal_stress": jnp.clip(jnp.exp(math.log(2.0) - 1.3862944 * jax.random.uniform(splits[4], (NX, NY), jnp.float32) ** steps_of(splits[4], (NX, NY), ((0, 8), (1, 4)), -0.2, 0.2)), 0.5, 2.0),
        "patch": with_ends(jax.random.randint(splits[5], (NX, NY), 0, PATCHES), jax.random.fold_in(splits[5], 1), 0, PATCHES - 1).astype(jnp.int32),
        "rate_coef": jnp.clip(jnp.exp(jax.random.uniform(splits[6], (PATCHES,), jnp.float32, math.log(0.3), math.log(1.0))), 0.3, 1.0),
        "state_coef": jnp.clip(jnp.exp(jax.random.uniform(splits[7], (PATCHES,), jnp.float32, math.log(0.3), math.log(1.0))), 0.3, 1.0),
        "slip_scale": jnp.clip(jnp.exp(jax.random.uniform(splits[8], (PATCHES,), jnp.float32, math.log(0.5), math.log(2.0))), 0.5, 2.0),
        "kernel": bell_draw(splits[9], (HIST, NY, NX), HIST ** -0.5, 1.5, ((1, 32),)),
        "history": bell_draw(splits[10], (HIST, 2, NY, NX), 1.0, 6.0, ((2, 32),)),
    }


shear_modulus = 1.0
damping = 0.5
relaxation = 0.35
time_step = 0.1

def inverse_sinh(value):
    size_v = jnp.abs(value)
    square = size_v * size_v
    result = jnp.log1p(size_v + square / (1.0 + jnp.sqrt(square + 1.0)))
    return jnp.where(value < 0.0, -result, result)

def lookup(patch, table):
    result = jnp.zeros(patch.shape, jnp.float32)
    for label in range(PATCHES):
        result = jnp.where(patch == label, table[label], result)
    return result

def friction(slip_rate, state, loading, normal_stress, transfer, coef_a, coef_b, length_l):
    stress = loading + transfer
    prefix = 2.0 * jnp.exp(-state / coef_a)
    angle_w = inverse_sinh(slip_rate / prefix)
    for iteration in range(NEWTON):
        residue = normal_stress * coef_a * angle_w + damping * prefix * jnp.sinh(angle_w) - stress
        slope = normal_stress * coef_a + damping * prefix * jnp.cosh(angle_w)
        ratio = residue / slope
        angle_w = angle_w - relaxation * ratio / (1.0 + jnp.abs(ratio))
    new_rate = prefix * jnp.sinh(angle_w)
    new_state = state + time_step * (coef_b / length_l) * (jnp.exp(-state / coef_b) - jnp.abs(new_rate))
    return (new_rate, new_state)

def wavenumber(count):
    index = jnp.arange(count, dtype=jnp.int32)
    return 2.0 * math.pi / count * ((index + count // 2) % count - count // 2).astype(jnp.float32)

def reference(slip, slip_rate, state, loading, normal_stress, patch, rate_coef, state_coef, slip_scale, kernel, history):
    slip_hat = jnp.fft.fft2(slip, norm='ortho').T
    rate_hat = jnp.fft.fft2(slip_rate, norm='ortho').T
    wave_x = wavenumber(NX)
    wave_y = wavenumber(NY)
    magnitude = jnp.sqrt(wave_y[:, None] ** 2 + wave_x[None, :] ** 2)
    kernel_full = kernel.astype(jnp.float32)
    memory_re = jnp.einsum('jrc,jrc->rc', kernel_full, history[:, 0].astype(jnp.float32))
    memory_im = jnp.einsum('jrc,jrc->rc', kernel_full, history[:, 1].astype(jnp.float32))
    static = -0.5 * shear_modulus * magnitude
    stress_re = static * jnp.real(slip_hat).astype(jnp.float32) + memory_re
    stress_im = static * jnp.imag(slip_hat).astype(jnp.float32) + memory_im
    stress_hat = (stress_re + 1j * stress_im).T
    transfer = jnp.real(jnp.fft.ifft2(stress_hat, norm='ortho')).astype(jnp.float32)
    rate_modes = jnp.stack([jnp.real(rate_hat), jnp.imag(rate_hat)]).astype(jnp.bfloat16)
    coef_a = lookup(patch, rate_coef)
    coef_b = lookup(patch, state_coef)
    length_l = lookup(patch, slip_scale)
    new_rate, new_state = friction(slip_rate, state, loading, normal_stress, transfer, coef_a, coef_b, length_l)
    return (new_rate, new_state, transfer, rate_modes)
```

```python
import math

import jax
import jax.numpy as jnp
from jax import lax
from jax.sharding import PartitionSpec as P

NEWTON = 8


shear_modulus = 1.0
damping = 0.5
relaxation = 0.35
time_step = 0.1


def inverse_sinh(value):
    size_v = jnp.abs(value)
    square = size_v * size_v
    result = jnp.log1p(size_v + square / (1.0 + jnp.sqrt(square + 1.0)))
    return jnp.where(value < 0.0, -result, result)


def exact_tables(rows, cols, modulus, sign):
    angles = 2.0 * math.pi / modulus * (rows * cols % modulus).astype(jnp.float32)
    return (jnp.cos(angles), sign * jnp.sin(angles))


def grid_tables(count_in, count_out, modulus, sign):
    row_index = lax.broadcasted_iota(jnp.int32, (count_in, count_out), 0)
    col_index = lax.broadcasted_iota(jnp.int32, (count_in, count_out), 1)
    return exact_tables(row_index, col_index, modulus, sign)


def complex_table(count, sign, scale=1.0):
    cos, sin = grid_tables(count, count, count, sign)
    cos, sin = cos * scale, sin * scale
    return jnp.stack([jnp.stack([cos, sin], 1), jnp.stack([-sin, cos], 1)], 0)


def product(pattern, left_op, right_op):
    return jnp.einsum(pattern, left_op, right_op, precision=lax.Precision.HIGH)


def twist(part_re, part_im, table_re, table_im):
    return (
        part_re * table_re - part_im * table_im,
        part_re * table_im + part_im * table_re,
    )


INNER = 128


def wavenumber(index, count):
    return 2.0 * math.pi / count * ((index + count // 2) % count - count // 2).astype(jnp.float32)


def lookup(patch, table):
    result = jnp.zeros(patch.shape, jnp.float32)
    for label in range(table.shape[0]):
        result = jnp.where(patch == label, table[label], result)
    return result


def friction(slip_rate, state, loading, normal_stress, transfer, coef_a, coef_b, length_l):
    stress = loading + transfer
    prefix = 2.0 * jnp.exp(-state / coef_a)
    angle_w = inverse_sinh(slip_rate / prefix)
    weight = normal_stress * coef_a
    half = 0.5 * damping * prefix
    for iteration in range(NEWTON):
        grow = half * jnp.exp(angle_w)
        decay = half * jnp.exp(-angle_w)
        residue = weight * angle_w + (grow - decay) - stress
        slope = weight + (grow + decay)
        angle_w = angle_w - relaxation * residue / (slope + jnp.abs(residue))
    new_rate = prefix * jnp.sinh(angle_w)
    new_state = state + time_step * (coef_b / length_l) * (
        jnp.exp(-state / coef_b) - jnp.abs(new_rate)
    )
    return (new_rate, new_state)


def real_rows(piece, total):
    sources, rows, chunk = piece.shape
    outer = total // INNER
    part = piece.reshape(sources, rows, chunk // INNER, INNER)
    table = jnp.stack(grid_tables(outer, outer, outer, -1.0), 1)
    table = table.reshape(sources, chunk // INNER, 2, outer)
    first = product("zrab,zakc->krcb", part, table)
    twist_re, twist_im = grid_tables(outer, INNER, total, -1.0)
    first = jnp.concatenate(twist(first[0], first[1], twist_re, twist_im), -1)
    second = complex_table(INNER, -1.0, 1.0 / math.sqrt(total))
    second = second.reshape(2 * INNER, 2, INNER)
    return [
        product("rcb,bm->mcr", first, second[:, part]).reshape(total, rows) for part in range(2)
    ]


def band_rows(part_re, part_im, sign):
    rows, total = part_re.shape
    outer = total // INNER
    table = complex_table(outer, sign).reshape(2 * outer, 2, outer)
    both = jnp.concatenate(
        [part_re.reshape(rows, outer, INNER), part_im.reshape(rows, outer, INNER)], 1
    )
    first = product("rab,akc->krcb", both, table)
    twist_re, twist_im = grid_tables(outer, INNER, total, sign)
    first = jnp.concatenate(twist(first[0], first[1], twist_re, twist_im), -1)
    second = complex_table(INNER, sign, 1.0 / math.sqrt(total)).reshape(2 * INNER, 2, INNER)
    return [
        product("rcb,bm->rmc", first, second[:, part]).reshape(rows, total) for part in range(2)
    ]


def real_cols(part_re, part_im):
    total, rows = part_re.shape
    outer = total // INNER
    both = jnp.concatenate(
        [part_re.reshape(outer, INNER, rows), part_im.reshape(outer, INNER, rows)], 0
    )
    table = complex_table(outer, 1.0).reshape(2 * outer, 2, outer)
    first = product("abr,akc->kcbr", both, table)
    twist_re, twist_im = grid_tables(outer, INNER, total, 1.0)
    first = jnp.concatenate(
        twist(first[0], first[1], twist_re[:, :, None], twist_im[:, :, None]), 1
    )
    second = complex_table(INNER, 1.0, 1.0 / math.sqrt(total)).reshape(2 * INNER, 2, INNER)
    return product("cbr,bm->rmc", first, second[:, 0]).reshape(rows, total)


def per_device(
    slip,
    slip_rate,
    state,
    loading,
    normal_stress,
    patch,
    rate_coef,
    state_coef,
    slip_scale,
    kernel,
    history,
):
    strike_count = lax.axis_size("strike")
    dip_count = lax.axis_size("dip")
    count = strike_count * dip_count
    both_axes = ("strike", "dip")
    cells_x, cells_y = slip.shape
    band, total_x = kernel.shape[1:]
    total_y = cells_y * dip_count
    rows = cells_x // dip_count
    keep = band // 2 + 1

    def gather_rows(array):
        return lax.all_to_all(
            array.reshape(dip_count, rows, cells_y), "dip", split_axis=0, concat_axis=0, tiled=True
        )

    def to_bands(part):
        return lax.all_to_all(part, both_axes, split_axis=0, concat_axis=1, tiled=True)

    slip_parts = real_rows(gather_rows(slip), total_y)
    rate_parts = real_rows(gather_rows(slip_rate), total_y)
    slip_parts = [part.reshape(count, band, rows)[:, :keep] for part in slip_parts]
    slip_both = jnp.concatenate(slip_parts, 1).reshape(count * 2 * keep, rows)
    slip_both = to_bands(slip_both)
    rate_parts = [to_bands(part) for part in rate_parts]
    slip_re, slip_im = band_rows(slip_both[:keep], slip_both[keep:], -1.0)
    rate_re, rate_im = band_rows(rate_parts[0], rate_parts[1], -1.0)
    rate_modes = jnp.stack([rate_re, rate_im]).astype(jnp.bfloat16)
    offset = (lax.axis_index("strike") * dip_count + lax.axis_index("dip")) * band
    row_index = lax.broadcasted_iota(jnp.int32, (keep,), 0)
    wave_y = wavenumber(offset + row_index, total_y)
    wave_x = wavenumber(lax.broadcasted_iota(jnp.int32, (total_x,), 0), total_x)
    magnitude = jnp.sqrt(wave_y[:, None] ** 2 + wave_x[None, :] ** 2)
    times = jnp.where((row_index == 0) | (row_index == band // 2), 1.0, 2.0)
    static = -0.5 * shear_modulus * magnitude * times[:, None]
    memory_re = jnp.einsum("jrc,jrc->rc", kernel, history[:, 0], preferred_element_type=jnp.float32)
    memory_im = jnp.einsum("jrc,jrc->rc", kernel, history[:, 1], preferred_element_type=jnp.float32)
    fill = ((0, band - keep), (0, 0))
    stress_re = jnp.pad(static * slip_re, fill) + memory_re
    stress_im = jnp.pad(static * slip_im, fill) + memory_im
    back = [
        lax.all_to_all(part, both_axes, split_axis=1, concat_axis=0, tiled=True)
        for part in band_rows(stress_re, stress_im, 1.0)
    ]
    line = real_cols(back[0], back[1])
    transfer = lax.all_to_all(line, "dip", split_axis=1, concat_axis=0, tiled=True)
    coef_a = lookup(patch, rate_coef)
    coef_b = lookup(patch, state_coef)
    length_l = lookup(patch, slip_scale)
    new_rate, new_state = friction(
        slip_rate, state, loading, normal_stress, transfer, coef_a, coef_b, length_l
    )
    return (new_rate, new_state, transfer, rate_modes)


def solution(mesh):
    return jax.shard_map(
        per_device,
        mesh=mesh,
        in_specs=(
            P("strike", "dip"),
            P("strike", "dip"),
            P("strike", "dip"),
            P("strike", "dip"),
            P("strike", "dip"),
            P("strike", "dip"),
            P(),
            P(),
            P(),
            P(None, ("strike", "dip"), None),
            P(None, None, ("strike", "dip"), None),
        ),
        out_specs=(
            P("strike", "dip"),
            P("strike", "dip"),
            P("strike", "dip"),
            P(None, ("strike", "dip"), None),
        ),
        check_vma=False,
    )
```

```python
import functools
import math

import jax
import jax.numpy as jnp
from jax import lax
from jax.experimental import pallas as pl
from jax.experimental.pallas import tpu as pltpu
from jax.sharding import PartitionSpec as P

NEWTON = 8


shear_modulus = 1.0
damping = 0.5
relaxation = 0.35
time_step = 0.1


def inverse_sinh(value):
    size_v = jnp.abs(value)
    square = size_v * size_v
    result = jnp.log1p(size_v + square / (1.0 + jnp.sqrt(square + 1.0)))
    return jnp.where(value < 0.0, -result, result)


def exact_tables(rows, cols, modulus, sign):
    angles = 2.0 * math.pi / modulus * (rows * cols % modulus).astype(jnp.float32)
    return (jnp.cos(angles), sign * jnp.sin(angles))


def grid_tables(count_in, count_out, modulus, sign):
    row_index = lax.broadcasted_iota(jnp.int32, (count_in, count_out), 0)
    col_index = lax.broadcasted_iota(jnp.int32, (count_in, count_out), 1)
    return exact_tables(row_index, col_index, modulus, sign)


def complex_table(count, sign, scale=1.0):
    cos, sin = grid_tables(count, count, count, sign)
    cos, sin = cos * scale, sin * scale
    return jnp.stack([jnp.stack([cos, sin], 1), jnp.stack([-sin, cos], 1)], 0)


def product(pattern, left_op, right_op):
    return jnp.einsum(pattern, left_op, right_op, precision=lax.Precision.HIGH)


def twist(part_re, part_im, table_re, table_im):
    return (
        part_re * table_re - part_im * table_im,
        part_re * table_im + part_im * table_re,
    )


INNER = 128


def wavenumber(index, count):
    return 2.0 * math.pi / count * ((index + count // 2) % count - count // 2).astype(jnp.float32)


def friction_kernel(
    labels,
    filled,
    rate_coef,
    state_coef,
    slip_scale,
    transfer_in,
    slip_rate_in,
    state_in,
    loading_in,
    normal_in,
    patch_in,
    *refs,
):
    new_rate_out, new_state_out, transfer_out = refs[filled:]
    patch = patch_in[...]

    def choose(table):
        result = jnp.zeros(patch.shape, jnp.float32)
        for label in range(labels):
            result = jnp.where(patch == label, table[label], result)
        return result

    coef_a = choose(rate_coef)
    coef_b = choose(state_coef)
    length_l = choose(slip_scale)
    transfer = transfer_in[0]
    state = state_in[...]
    stress = loading_in[...] + transfer
    prefix = 2.0 * jnp.exp(-state / coef_a)
    angle_w = inverse_sinh(slip_rate_in[...] / prefix)
    weight = normal_in[...] * coef_a
    half = 0.5 * damping * prefix
    for iteration in range(NEWTON):
        grow = half * jnp.exp(angle_w)
        decay = half * jnp.exp(-angle_w)
        residue = weight * angle_w + (grow - decay) - stress
        slope = weight + (grow + decay)
        angle_w = angle_w - relaxation * residue / (slope + jnp.abs(residue))
    new_rate = (0.5 * prefix) * (jnp.exp(angle_w) - jnp.exp(-angle_w))
    new_rate_out[...] = new_rate
    new_state_out[...] = state + time_step * (coef_b / length_l) * (
        jnp.exp(-state / coef_b) - jnp.abs(new_rate)
    )
    transfer_out[...] = transfer


def friction(part, parts, tables, transfer, cells, before):
    sources, rows, columns = transfer.shape
    block = pl.BlockSpec((rows, columns), lambda step: (step * parts + part, 0))
    scalar = pl.BlockSpec(memory_space=pltpu.SMEM)
    size = transfer.size
    first = len(tables) + 1 + len(cells)
    return pl.pallas_call(
        functools.partial(friction_kernel, tables[0].shape[0], len(before)),
        grid=(sources,),
        out_shape=[jax.ShapeDtypeStruct(cells[0].shape, jnp.float32)] * 3,
        in_specs=[scalar] * len(tables)
        + [pl.BlockSpec((1, rows, columns), lambda step: (step, 0, 0))]
        + [block] * len(cells)
        + [pl.BlockSpec(memory_space=pl.ANY)] * len(before),
        out_specs=[block] * 3,
        input_output_aliases={first + index: index for index in range(len(before))},
        compiler_params=pltpu.CompilerParams(vmem_limit_bytes=32 * 1024 * 1024),
        cost_estimate=pl.CostEstimate(
            flops=size * 200, bytes_accessed=size * 36, transcendentals=size * 30
        ),
    )(*tables, transfer, *cells, *before)


def real_rows(piece, total):
    sources, rows, chunk = piece.shape
    outer = total // INNER
    part = piece.reshape(sources, rows, chunk // INNER, INNER)
    table = jnp.stack(grid_tables(outer, outer, outer, -1.0), 1)
    table = table.reshape(sources, chunk // INNER, 2, outer)
    first = product("zrab,zakc->krcb", part, table)
    twist_re, twist_im = grid_tables(outer, INNER, total, -1.0)
    first = jnp.concatenate(twist(first[0], first[1], twist_re, twist_im), -1)
    second = complex_table(INNER, -1.0, 1.0 / math.sqrt(total))
    second = second.reshape(2 * INNER, 2, INNER)
    return [
        product("rcb,bm->mcr", first, second[:, part]).reshape(total, rows) for part in range(2)
    ]


def band_rows(part_re, part_im, sign):
    rows, total = part_re.shape
    outer = total // INNER
    table = complex_table(outer, sign).reshape(2 * outer, 2, outer)
    both = jnp.concatenate(
        [part_re.reshape(rows, outer, INNER), part_im.reshape(rows, outer, INNER)], 1
    )
    first = product("rab,akc->krcb", both, table)
    twist_re, twist_im = grid_tables(outer, INNER, total, sign)
    first = jnp.concatenate(twist(first[0], first[1], twist_re, twist_im), -1)
    second = complex_table(INNER, sign, 1.0 / math.sqrt(total)).reshape(2 * INNER, 2, INNER)
    return [
        product("rcb,bm->rmc", first, second[:, part]).reshape(rows, total) for part in range(2)
    ]


def real_cols(part_re, part_im):
    total, rows = part_re.shape
    outer = total // INNER
    both = jnp.concatenate(
        [part_re.reshape(outer, INNER, rows), part_im.reshape(outer, INNER, rows)], 0
    )
    table = complex_table(outer, 1.0).reshape(2 * outer, 2, outer)
    first = product("abr,akc->kcbr", both, table)
    twist_re, twist_im = grid_tables(outer, INNER, total, 1.0)
    first = jnp.concatenate(
        twist(first[0], first[1], twist_re[:, :, None], twist_im[:, :, None]), 1
    )
    second = complex_table(INNER, 1.0, 1.0 / math.sqrt(total)).reshape(2 * INNER, 2, INNER)
    return product("cbr,bm->rmc", first, second[:, 0]).reshape(rows, total)


def per_device(
    slip,
    slip_rate,
    state,
    loading,
    normal_stress,
    patch,
    rate_coef,
    state_coef,
    slip_scale,
    kernel,
    history,
):
    strike_count = lax.axis_size("strike")
    dip_count = lax.axis_size("dip")
    count = strike_count * dip_count
    both_axes = ("strike", "dip")
    cells_x, cells_y = slip.shape
    band, total_x = kernel.shape[1:]
    total_y = cells_y * dip_count
    rows = cells_x // dip_count
    keep = band // 2 + 1

    def gather_rows(array):
        return lax.all_to_all(
            array.reshape(dip_count, rows, cells_y), "dip", split_axis=0, concat_axis=0, tiled=True
        )

    def to_bands(part):
        return lax.all_to_all(part, both_axes, split_axis=0, concat_axis=1, tiled=True)

    def after(value, earlier):
        return lax.optimization_barrier((value, earlier))

    def band_piece(pair, start, stop):
        pieces = [part.reshape(count, band, rows)[:, start:stop] for part in pair]
        return jnp.concatenate(pieces, 1).reshape(count * 2 * (stop - start), rows)

    def modes(piece):
        half = piece.shape[0] // 2
        return jnp.stack(band_rows(piece[:half], piece[half:], -1.0)).astype(jnp.bfloat16)

    slip_rows = gather_rows(slip)
    rate_rows, slip_rows = after(slip_rate, slip_rows)
    rate_rows = gather_rows(rate_rows)
    slip_parts = real_rows(slip_rows, total_y)
    slip_both, rate_rows = after(band_piece(slip_parts, 0, keep), rate_rows)
    slip_both = to_bands(slip_both)
    rate_parts = real_rows(rate_rows, total_y)
    cut = band - band // 4
    rate_first, slip_both = after(band_piece(rate_parts, 0, cut), slip_both)
    rate_first = to_bands(rate_first)
    slip_re, slip_im = band_rows(slip_both[:keep], slip_both[keep:], -1.0)
    offset = (lax.axis_index("strike") * dip_count + lax.axis_index("dip")) * band
    row_index = lax.broadcasted_iota(jnp.int32, (keep,), 0)
    wave_y = wavenumber(offset + row_index, total_y)
    wave_x = wavenumber(lax.broadcasted_iota(jnp.int32, (total_x,), 0), total_x)
    magnitude = jnp.sqrt(wave_y[:, None] ** 2 + wave_x[None, :] ** 2)
    times = jnp.where((row_index == 0) | (row_index == band // 2), 1.0, 2.0)
    static = -0.5 * shear_modulus * magnitude * times[:, None]
    memory_re = jnp.einsum("jrc,jrc->rc", kernel, history[:, 0], preferred_element_type=jnp.float32)
    memory_im = jnp.einsum("jrc,jrc->rc", kernel, history[:, 1], preferred_element_type=jnp.float32)
    fill = ((0, band - keep), (0, 0))
    stress_re = jnp.pad(static * slip_re, fill) + memory_re
    stress_im = jnp.pad(static * slip_im, fill) + memory_im
    back_parts = band_rows(stress_re, stress_im, 1.0)

    back = jnp.concatenate(back_parts, 0)
    back, rate_first = after(back, rate_first)
    back = lax.all_to_all(back, both_axes, split_axis=1, concat_axis=0, tiled=True)
    modes_first = modes(rate_first)
    rate_last, (back, modes_first) = after(
        band_piece(rate_parts, cut, band), (back, modes_first)
    )
    rate_last = to_bands(rate_last)
    back = back.reshape(count, 2, band, rows)
    line = real_cols(back[:, 0].reshape(total_y, rows), back[:, 1].reshape(total_y, rows))
    line, rate_last = after(line, rate_last)
    tables = (rate_coef, state_coef, slip_scale)
    cells = (slip_rate, state, loading, normal_stress, patch)
    parts = 2
    pieces = []
    for part in range(parts):
        piece = line[part * (rows // parts) : (part + 1) * (rows // parts)]
        piece = piece.reshape(rows // parts, dip_count, cells_y).transpose(1, 0, 2)
        if pieces:
            piece, pieces[-1] = after(piece, pieces[-1])
        pieces.append(lax.all_to_all(piece, "dip", split_axis=0, concat_axis=0, tiled=True))
    rate_modes = jnp.concatenate([modes_first, modes(rate_last)], 1)
    outs = []
    for part in range(parts):
        outs = friction(part, parts, tables, pieces[part], cells, outs)
    return (*outs, rate_modes)


def solution(mesh):
    return jax.shard_map(
        per_device,
        mesh=mesh,
        in_specs=(
            P("strike", "dip"),
            P("strike", "dip"),
            P("strike", "dip"),
            P("strike", "dip"),
            P("strike", "dip"),
            P("strike", "dip"),
            P(),
            P(),
            P(),
            P(None, ("strike", "dip"), None),
            P(None, None, ("strike", "dip"), None),
        ),
        out_specs=(
            P("strike", "dip"),
            P("strike", "dip"),
            P("strike", "dip"),
            P(None, ("strike", "dip"), None),
        ),
        check_vma=False,
    )
```

```python
import functools
import math

import jax
import jax.numpy as jnp
from jax import lax
from jax.experimental import pallas as pl
from jax.experimental.pallas import tpu as pltpu
from jax.sharding import PartitionSpec as P

NEWTON = 8


shear_modulus = 1.0
damping = 0.5
relaxation = 0.35
time_step = 0.1


def inverse_sinh(value):
    size_v = jnp.abs(value)
    square = size_v * size_v
    result = jnp.log1p(size_v + square / (1.0 + jnp.sqrt(square + 1.0)))
    return jnp.where(value < 0.0, -result, result)


def exact_tables(rows, cols, modulus, sign):
    angles = 2.0 * math.pi / modulus * (rows * cols % modulus).astype(jnp.float32)
    return (jnp.cos(angles), sign * jnp.sin(angles))


def grid_tables(count_in, count_out, modulus, sign):
    row_index = lax.broadcasted_iota(jnp.int32, (count_in, count_out), 0)
    col_index = lax.broadcasted_iota(jnp.int32, (count_in, count_out), 1)
    return exact_tables(row_index, col_index, modulus, sign)


def complex_table(count, sign, scale=1.0):
    cos, sin = grid_tables(count, count, count, sign)
    cos, sin = cos * scale, sin * scale
    return jnp.stack([jnp.stack([cos, sin], 1), jnp.stack([-sin, cos], 1)], 0)


def product(pattern, left_op, right_op):
    return jnp.einsum(pattern, left_op, right_op, precision=lax.Precision.HIGH)


def twist(part_re, part_im, table_re, table_im):
    return (
        part_re * table_re - part_im * table_im,
        part_re * table_im + part_im * table_re,
    )


INNER = 128


def wavenumber(index, count):
    return 2.0 * math.pi / count * ((index + count // 2) % count - count // 2).astype(jnp.float32)


def friction_kernel(
    labels,
    filled,
    rate_coef,
    state_coef,
    slip_scale,
    transfer_in,
    slip_rate_in,
    state_in,
    loading_in,
    normal_in,
    patch_in,
    *refs,
):
    new_rate_out, new_state_out, transfer_out = refs[filled:]
    patch = patch_in[...]

    def choose(table):
        result = jnp.zeros(patch.shape, jnp.float32)
        for label in range(labels):
            result = jnp.where(patch == label, table[label], result)
        return result

    coef_a = choose(rate_coef)
    coef_b = choose(state_coef)
    length_l = choose(slip_scale)
    transfer = transfer_in[0]
    state = state_in[...]
    stress = loading_in[...] + transfer
    prefix = 2.0 * jnp.exp(-state / coef_a)
    angle_w = inverse_sinh(slip_rate_in[...] / prefix)
    weight = normal_in[...] * coef_a
    half = 0.5 * damping * prefix
    for iteration in range(NEWTON):
        grow = half * jnp.exp(angle_w)
        decay = half * jnp.exp(-angle_w)
        residue = weight * angle_w + (grow - decay) - stress
        slope = weight + (grow + decay)
        angle_w = angle_w - relaxation * residue / (slope + jnp.abs(residue))
    new_rate = (0.5 * prefix) * (jnp.exp(angle_w) - jnp.exp(-angle_w))
    new_rate_out[...] = new_rate
    new_state_out[...] = state + time_step * (coef_b / length_l) * (
        jnp.exp(-state / coef_b) - jnp.abs(new_rate)
    )
    transfer_out[...] = transfer


def friction(part, parts, tables, transfer, cells, before):
    sources, rows, columns = transfer.shape
    block = pl.BlockSpec((rows, columns), lambda step: (step * parts + part, 0))
    scalar = pl.BlockSpec(memory_space=pltpu.SMEM)
    size = transfer.size
    first = len(tables) + 1 + len(cells)
    return pl.pallas_call(
        functools.partial(friction_kernel, tables[0].shape[0], len(before)),
        grid=(sources,),
        out_shape=[jax.ShapeDtypeStruct(cells[0].shape, jnp.float32)] * 3,
        in_specs=[scalar] * len(tables)
        + [pl.BlockSpec((1, rows, columns), lambda step: (step, 0, 0))]
        + [block] * len(cells)
        + [pl.BlockSpec(memory_space=pl.ANY)] * len(before),
        out_specs=[block] * 3,
        input_output_aliases={first + index: index for index in range(len(before))},
        compiler_params=pltpu.CompilerParams(vmem_limit_bytes=32 * 1024 * 1024),
        cost_estimate=pl.CostEstimate(
            flops=size * 200, bytes_accessed=size * 36, transcendentals=size * 30
        ),
    )(*tables, transfer, *cells, *before)


def real_rows(piece, total):
    sources, rows, chunk = piece.shape
    outer = total // INNER
    part = piece.reshape(sources, rows, chunk // INNER, INNER)
    table = jnp.stack(grid_tables(outer, outer, outer, -1.0), 1)
    table = table.reshape(sources, chunk // INNER, 2, outer)
    first = product("zrab,zakc->krcb", part, table)
    twist_re, twist_im = grid_tables(outer, INNER, total, -1.0)
    first = jnp.concatenate(twist(first[0], first[1], twist_re, twist_im), -1)
    second = complex_table(INNER, -1.0, 1.0 / math.sqrt(total))
    second = second.reshape(2 * INNER, 2, INNER)
    return [
        product("rcb,bm->mcr", first, second[:, part]).reshape(total, rows) for part in range(2)
    ]


def band_rows(part_re, part_im, sign):
    rows, total = part_re.shape
    outer = total // INNER
    table = complex_table(outer, sign).reshape(2 * outer, 2, outer)
    both = jnp.concatenate(
        [part_re.reshape(rows, outer, INNER), part_im.reshape(rows, outer, INNER)], 1
    )
    first = product("rab,akc->krcb", both, table)
    twist_re, twist_im = grid_tables(outer, INNER, total, sign)
    first = jnp.concatenate(twist(first[0], first[1], twist_re, twist_im), -1)
    second = complex_table(INNER, sign, 1.0 / math.sqrt(total)).reshape(2 * INNER, 2, INNER)
    return [
        product("rcb,bm->rmc", first, second[:, part]).reshape(rows, total) for part in range(2)
    ]


def real_cols(part_re, part_im):
    total, rows = part_re.shape
    outer = total // INNER
    both = jnp.concatenate(
        [part_re.reshape(outer, INNER, rows), part_im.reshape(outer, INNER, rows)], 0
    )
    table = complex_table(outer, 1.0).reshape(2 * outer, 2, outer)
    first = product("abr,akc->kcbr", both, table)
    twist_re, twist_im = grid_tables(outer, INNER, total, 1.0)
    first = jnp.concatenate(
        twist(first[0], first[1], twist_re[:, :, None], twist_im[:, :, None]), 1
    )
    second = complex_table(INNER, 1.0, 1.0 / math.sqrt(total)).reshape(2 * INNER, 2, INNER)
    return product("cbr,bm->rmc", first, second[:, 0]).reshape(rows, total)


def per_device(
    slip,
    slip_rate,
    state,
    loading,
    normal_stress,
    patch,
    rate_coef,
    state_coef,
    slip_scale,
    kernel,
    history,
):
    strike_count = lax.axis_size("strike")
    dip_count = lax.axis_size("dip")
    count = strike_count * dip_count
    both_axes = ("strike", "dip")
    cells_x, cells_y = slip.shape
    band, total_x = kernel.shape[1:]
    total_y = cells_y * dip_count
    rows = cells_x // dip_count
    keep = band // 2 + 1

    def gather_rows(array):
        return lax.all_to_all(
            array.reshape(dip_count, rows, cells_y), "dip", split_axis=0, concat_axis=0, tiled=True
        )

    def to_bands(part):
        piece = lax.all_to_all(part, both_axes, split_axis=0, concat_axis=0, tiled=True)
        return piece.transpose(1, 0, 2).reshape(piece.shape[1], count * rows)

    def after(value, earlier):
        return lax.optimization_barrier((value, earlier))

    def band_piece(pair, start, stop):
        pieces = [part.reshape(count, band, rows)[:, start:stop] for part in pair]
        return jnp.concatenate(pieces, 1)

    def modes(piece):
        half = piece.shape[0] // 2
        return jnp.stack(band_rows(piece[:half], piece[half:], -1.0)).astype(jnp.bfloat16)

    slip_rows = gather_rows(slip)
    rate_rows, slip_rows = after(slip_rate, slip_rows)
    rate_rows = gather_rows(rate_rows)
    slip_parts = real_rows(slip_rows, total_y)
    slip_both, rate_rows = after(band_piece(slip_parts, 0, keep), rate_rows)
    slip_both = to_bands(slip_both)
    rate_parts = real_rows(rate_rows, total_y)
    cut = band - band // 4
    rate_first, slip_both = after(band_piece(rate_parts, 0, cut), slip_both)
    rate_first = to_bands(rate_first)
    slip_re, slip_im = band_rows(slip_both[:keep], slip_both[keep:], -1.0)
    offset = (lax.axis_index("strike") * dip_count + lax.axis_index("dip")) * band
    row_index = lax.broadcasted_iota(jnp.int32, (keep,), 0)
    wave_y = wavenumber(offset + row_index, total_y)
    wave_x = wavenumber(lax.broadcasted_iota(jnp.int32, (total_x,), 0), total_x)
    magnitude = jnp.sqrt(wave_y[:, None] ** 2 + wave_x[None, :] ** 2)
    times = jnp.where((row_index == 0) | (row_index == band // 2), 1.0, 2.0)
    static = -0.5 * shear_modulus * magnitude * times[:, None]
    memory_re = jnp.einsum("jrc,jrc->rc", kernel, history[:, 0], preferred_element_type=jnp.float32)
    memory_im = jnp.einsum("jrc,jrc->rc", kernel, history[:, 1], preferred_element_type=jnp.float32)
    fill = ((0, band - keep), (0, 0))
    stress_re = jnp.pad(static * slip_re, fill) + memory_re
    stress_im = jnp.pad(static * slip_im, fill) + memory_im
    back_parts = band_rows(stress_re, stress_im, 1.0)

    back = jnp.concatenate(back_parts, 0).reshape(2 * band, count, rows).transpose(1, 0, 2)
    back, rate_first = after(back, rate_first)
    back = lax.all_to_all(back, both_axes, split_axis=0, concat_axis=0, tiled=True)
    modes_first = modes(rate_first)
    rate_last, (back, modes_first) = after(
        band_piece(rate_parts, cut, band), (back, modes_first)
    )
    rate_last = to_bands(rate_last)
    back = back.reshape(count, 2, band, rows)
    line = real_cols(back[:, 0].reshape(total_y, rows), back[:, 1].reshape(total_y, rows))
    line, rate_last = after(line, rate_last)
    tables = (rate_coef, state_coef, slip_scale)
    cells = (slip_rate, state, loading, normal_stress, patch)
    parts = 2
    pieces = []
    for part in range(parts):
        piece = line[part * (rows // parts) : (part + 1) * (rows // parts)]
        piece = piece.reshape(rows // parts, dip_count, cells_y).transpose(1, 0, 2)
        if pieces:
            piece, pieces[-1] = after(piece, pieces[-1])
        pieces.append(lax.all_to_all(piece, "dip", split_axis=0, concat_axis=0, tiled=True))
    rate_modes = jnp.concatenate([modes_first, modes(rate_last)], 1)
    outs = []
    for part in range(parts):
        outs = friction(part, parts, tables, pieces[part], cells, outs)
    return (*outs, rate_modes)


def solution(mesh):
    return jax.shard_map(
        per_device,
        mesh=mesh,
        in_specs=(
            P("strike", "dip"),
            P("strike", "dip"),
            P("strike", "dip"),
            P("strike", "dip"),
            P("strike", "dip"),
            P("strike", "dip"),
            P(),
            P(),
            P(),
            P(None, ("strike", "dip"), None),
            P(None, None, ("strike", "dip"), None),
        ),
        out_specs=(
            P("strike", "dip"),
            P("strike", "dip"),
            P("strike", "dip"),
            P(None, ("strike", "dip"), None),
        ),
        check_vma=False,
    )
```
